32 devices in a mesh: mem: 4 (over y, core), kvh: 4 (over z), row: 2 (over x).
Axes of the slice: x: 2, y: 2, z: 4, core: 2. Of those that a mesh axis runs over, the one named last changes fastest.
Arguments:
- queries: bfloat16 [64, 8192], P(('mem', 'kvh', 'row')), may hold values from -120 to 120
- output_gradient: bfloat16 [64, 8192], P(('mem', 'kvh', 'row')), may hold values from -6 to 6
- keys: bfloat16 [3072, 1024], P('mem', 'kvh'), may hold values from -6 to 6
- values: bfloat16 [3072, 1024], P('mem', 'kvh'), may hold values from -6 to 6
- text_video: int32 [16, 4], P(None, 'row'), may hold values from 0 to 11
- video_blocks: int32 [12], replicated, may hold values from 1 to 4, 24 in all
Outputs:
- attention_out: bfloat16 [64, 8192], P(('mem', 'kvh', 'row'))
- query_grad: bfloat16 [64, 8192], P(('mem', 'kvh', 'row'))
- keys_gradient: bfloat16 [3072, 1024], P('mem', 'kvh')
- values_gradient: bfloat16 [3072, 1024], P('mem', 'kvh')
The draws below stay inside these ranges and needn't reach their ends.
Inputs may be any that keep to these rules, and one draw needn't show every extreme that they name: Row sees images 0 to text_video. `video_blocks`: they sum to 24.
All inputs are finite; a program needn't handle non-finite values.
Results may differ from the reference program's by a relative error of at most 0.015.
Values may be sent and summed in bfloat16 or wider, within the bound.
No kernel may reach another device: no remote copies, remote signals or barrier semaphores. Data moves between devices by JAX's collectives and lax.ppermute only.
A program may use at most 64 MiB of HBM per device.

```python
import math
import jax
import jax.numpy as jnp
import numpy as np
from jax import lax

QUERY_HEADS = 64
KEY_VALUE_HEADS = 8
HEAD_WIDTH = 128
FRAME = 128
ROW_DEV = 2
TEXT_ROW_COUNT = 64
VISUAL_TOKENS = 3072
BLOCKS = 24
VIDEOS = 12
N_MEM = 4
N_KVH = 4
N_ROW = 2


def drawn_pair(key):
    base_key = jax.random.fold_in(key, 4099)
    key_query, random_key_seeds = jax.random.split(base_key, 2)
    queries = jnp.clip(2.0 * jax.random.normal(key_query, (TEXT_ROW_COUNT, QUERY_HEADS, HEAD_WIDTH), jnp.float32), -12.0, 12.0)
    keys = jnp.clip(jax.random.normal(random_key_seeds, (VISUAL_TOKENS, KEY_VALUE_HEADS, HEAD_WIDTH), jnp.float32), -6.0, 6.0)
    return (queries.reshape(TEXT_ROW_COUNT, QUERY_HEADS * HEAD_WIDTH), keys.reshape(VISUAL_TOKENS, KEY_VALUE_HEADS * HEAD_WIDTH))


def draw_queries(key, part):
    return drawn_pair(key)[0].astype(jnp.bfloat16)


def draw_keys(key, part):
    return drawn_pair(key)[1].astype(jnp.bfloat16)


def plant(values, rng, low, largest):
    dims = values.shape
    index_at = [jax.random.randint(jax.random.fold_in(rng, axis), (), 0, dims[axis]) for axis in range(len(dims))]
    values = values.at[tuple(index_at)].set(low)
    longest = dims.index(max(dims))
    index_at[longest] = (index_at[longest] + 1) % dims[longest]
    return values.at[tuple(index_at)].set(largest)


def shard_levels(stream_key, shape, pieces, low, high):
    def one(position, blocks):
        steps = jax.random.uniform(jax.random.fold_in(jax.random.fold_in(stream_key, 6), position), (blocks,), jnp.float32, low / len(pieces), high / len(pieces))
        return jnp.repeat(jnp.exp(steps), shape[position] // blocks).reshape((-1,) + (1,) * (len(shape) - position - 1))

    loudness = one(*pieces[0])
    for cut in pieces[1:]:
        loudness = loudness * one(*cut)
    return loudness


def profile(number_of, total, bound, slope):
    weights = [(1 << 20) // math.isqrt(rank ** slope) + 1 for rank in range(2, number_of + 1)]
    rest, given = total - bound - (number_of - 1), [1] * (number_of - 1)
    while rest > 0:
        candidates = [i for i in range(number_of - 1) if given[i] < bound]
        mass, remaining = sum([weights[i] for i in candidates]), rest
        for i in candidates:
            extra = min(bound - given[i], max(1, remaining * weights[i] // mass), rest)
            given[i] = given[i] + extra
            rest = rest - extra
    return np.array([bound] + given)


def ragged_sizes(rng, number_of, total, most, lean):
    if number_of == 2:
        one = jax.random.randint(rng, (), max(1, total - most), min(most, total - 1) + 1)
        return jnp.stack([one, total - one])
    lengths = jnp.asarray(profile(number_of, total, most, lean), jnp.int32)
    pairs = (number_of - 1) // 2
    source_of, sink = lengths[1:1 + 2 * pairs:2], lengths[2:2 + 2 * pairs:2]
    margin = jnp.minimum(source_of - 1, most - sink)
    passed = jax.random.randint(jax.random.fold_in(rng, 1), (pairs,), 0, 1 << 20) % (margin + 1)
    lengths = lengths.at[1:1 + 2 * pairs:2].set(source_of - passed).at[2:2 + 2 * pairs:2].set(sink + passed)
    return lengths[jax.random.permutation(jax.random.fold_in(rng, 2), number_of)]


def gaussian(rng, extent, scale, bound, cuts=(), kind=jnp.bfloat16):
    array = jax.random.normal(rng, extent, jnp.float32) * scale
    if len(cuts) > 0:
        array = shard_levels(rng, extent, cuts, -0.22, 0.18) * array
    return jnp.clip(array, min=-bound, max=bound).astype(kind)


def setup_inputs(seed: int = 0) -> dict:
    arg_keys = jax.random.split(jax.random.key(seed), 7)
    return {
        "queries": draw_queries(jax.random.fold_in(arg_keys[6], 71), 0),
        "output_gradient": gaussian(arg_keys[1], (TEXT_ROW_COUNT, QUERY_HEADS * HEAD_WIDTH), 1.0, 6.0, ((0, 32),)),
        "keys": draw_keys(jax.random.fold_in(arg_keys[6], 71), 0),
        "values": gaussian(arg_keys[3], (VISUAL_TOKENS, KEY_VALUE_HEADS * HEAD_WIDTH), 1.0, 6.0, ((0, 4), (1, 4))),
        "text_video": plant(jax.random.randint(arg_keys[4], (N_MEM * N_KVH, N_ROW * ROW_DEV), 0, VIDEOS), jax.random.fold_in(arg_keys[4], 1), 0, VIDEOS - 1).astype(jnp.int32),
        "video_blocks": ragged_sizes(arg_keys[5], VIDEOS, BLOCKS, 4, 2).astype(jnp.int32),
    }


masked_score = -1.0e30


def video_of_block(video_blocks, block_count):
    block_ends = jnp.cumsum(video_blocks)
    blocks = jnp.arange(block_count, dtype=jnp.int32)
    return jnp.sum((block_ends[None, :] <= blocks[:, None]).astype(jnp.int32), axis=1)


def one_head(query, gradient, key_head, value_head, visible):
    inverse_root = HEAD_WIDTH ** -0.5
    scores = jnp.dot(query, key_head.T, preferred_element_type=jnp.float32) * inverse_root
    scores = jnp.where(visible, scores, masked_score)
    row_top = jnp.max(scores, axis=1, keepdims=True)
    weight = jnp.where(visible, jnp.exp(scores - row_top), 0.0)
    totals = jnp.sum(weight, axis=1, keepdims=True)
    attention = jnp.dot(weight.astype(jnp.bfloat16), value_head, preferred_element_type=jnp.float32) / totals
    log_mass = row_top + jnp.log(totals)
    probability = jnp.where(visible, jnp.exp(scores - log_mass), 0.0)
    delta = jnp.sum(gradient.astype(jnp.float32) * attention, axis=1, keepdims=True)
    prob_grad = jnp.dot(gradient, value_head.T, preferred_element_type=jnp.float32)
    score_grad = (probability * (prob_grad - delta)).astype(jnp.bfloat16)
    query_grad = jnp.dot(score_grad, key_head, preferred_element_type=jnp.float32) * inverse_root
    keys_gradient = jnp.dot(score_grad.T, query, preferred_element_type=jnp.float32) * inverse_root
    values_gradient = jnp.dot(probability.astype(jnp.bfloat16).T, gradient, preferred_element_type=jnp.float32)
    return attention, query_grad, keys_gradient, values_gradient


def reference(queries, output_gradient, keys, values, text_video, video_blocks):
    key_video = jnp.repeat(video_of_block(video_blocks, VISUAL_TOKENS // FRAME), FRAME)
    visible = key_video[None, :] <= text_video.reshape(TEXT_ROW_COUNT)[:, None]
    heads_per_group = QUERY_HEADS // KEY_VALUE_HEADS
    query_pieces = queries.reshape(TEXT_ROW_COUNT, KEY_VALUE_HEADS, heads_per_group, HEAD_WIDTH).transpose(1, 2, 0, 3)
    gradient_pieces = output_gradient.reshape(TEXT_ROW_COUNT, KEY_VALUE_HEADS, heads_per_group, HEAD_WIDTH).transpose(1, 2, 0, 3)
    key_pieces = keys.reshape(VISUAL_TOKENS, KEY_VALUE_HEADS, HEAD_WIDTH).transpose(1, 0, 2)
    value_pieces = values.reshape(VISUAL_TOKENS, KEY_VALUE_HEADS, HEAD_WIDTH).transpose(1, 0, 2)

    def per_key_head(inputs):
        query_group, grad_group, key_head, value_head = inputs

        def per_query_head(pair_in):
            return one_head(pair_in[0], pair_in[1], key_head, value_head, visible)

        attention, query_grad, keys_gradient, values_gradient = lax.map(per_query_head, (query_group, grad_group))
        return attention, query_grad, jnp.sum(keys_gradient, axis=0), jnp.sum(values_gradient, axis=0)

    attention, query_grad, keys_gradient, values_gradient = lax.map(per_key_head, (query_pieces, gradient_pieces, key_pieces, value_pieces))
    attention_out = attention.transpose(2, 0, 1, 3).reshape(TEXT_ROW_COUNT, QUERY_HEADS * HEAD_WIDTH).astype(jnp.bfloat16)
    query_out = query_grad.transpose(2, 0, 1, 3).reshape(TEXT_ROW_COUNT, QUERY_HEADS * HEAD_WIDTH).astype(jnp.bfloat16)
    keys_result = keys_gradient.transpose(1, 0, 2).reshape(VISUAL_TOKENS, KEY_VALUE_HEADS * HEAD_WIDTH).astype(jnp.bfloat16)
    values_result = values_gradient.transpose(1, 0, 2).reshape(VISUAL_TOKENS, KEY_VALUE_HEADS * HEAD_WIDTH).astype(jnp.bfloat16)
    return (attention_out, query_out, keys_result, values_result)
```

```python
import functools
import math

import jax
import jax.numpy as jnp
from jax import lax
from jax.experimental import pallas as pl
from jax.experimental.pallas import tpu as pltpu
from jax.sharding import PartitionSpec as P

QUERY_HEADS = 64
KEY_VALUE_HEADS = 8
HEAD_WIDTH = 128
FRAME = 128
GROUP = QUERY_HEADS // KEY_VALUE_HEADS


masked_score = -1e30
hidden = 1e30
inverse_root = HEAD_WIDTH ** (-0.5)
exp2_scale = inverse_root * math.log2(math.e)

NT = (((1,), (1,)), ((), ()))
NN = (((1,), (0,)), ((), ()))
TN = (((0,), (0,)), ((), ()))
VM = pl.BlockSpec(memory_space=pltpu.VMEM)
SM = pl.BlockSpec(memory_space=pltpu.SMEM)
f32 = jnp.float32
bf16 = jnp.bfloat16


def dot(a, b, dims):
    return lax.dot_general(a, b, dims, preferred_element_type=f32)


def call(body, outs, specs, scratch=(), flops=0, exps=0, moved=0):
    return pl.pallas_call(
        body,
        out_shape=outs,
        in_specs=specs,
        out_specs=jax.tree.map(lambda _: VM, outs),
        scratch_shapes=list(scratch),
        cost_estimate=pl.CostEstimate(
            flops=flops, transcendentals=exps, bytes_accessed=moved
        ),
        compiler_params=pltpu.CompilerParams(vmem_limit_bytes=48 << 20),
    )


def split_columns(parts, rows, where, q_ref, g_ref, *rest):
    outs, tmp = rest[:parts], rest[parts]
    heads = q_ref.shape[1] // HEAD_WIDTH // parts
    own = where[0]
    for d in range(parts):
        base = (own ^ d) * (heads * HEAD_WIDTH)
        for n, ref in enumerate((q_ref, g_ref)):
            for h in range(heads):
                at = pl.multiple_of(base + h * HEAD_WIDTH, HEAD_WIDTH)
                line = (n * heads + h) * rows
                tmp[line : line + rows, :] = ref[:, pl.ds(at, HEAD_WIDTH)].astype(f32)
        outs[d][...] = tmp[...].astype(bf16)


def join_columns(parts, rows, where, *rest):
    blocks, a_ref, q_ref, tmp = rest[:parts], rest[parts], rest[parts + 1], rest[parts + 2]
    heads = q_ref.shape[1] // HEAD_WIDTH // parts
    own = where[0]
    for d in range(parts):
        tmp[...] = blocks[d][...].astype(f32)
        base = (own ^ d) * (heads * HEAD_WIDTH)
        for n, ref in enumerate((a_ref, q_ref)):
            for h in range(heads):
                at = pl.multiple_of(base + h * HEAD_WIDTH, HEAD_WIDTH)
                line = (n * heads + h) * rows
                ref[:, pl.ds(at, HEAD_WIDTH)] = tmp[line : line + rows, :].astype(bf16)


def visibility(sizes, where, blocks_ref, *rest):
    row_n, core_n, far_n, kvh_n, rows, frames = sizes
    texts, out = rest[:row_n], rest[row_n]
    kvh, mem = where[0], where[1]
    lanes = out.shape[1]
    per = GROUP * rows
    lane = lax.broadcasted_iota(jnp.int32, (1, lanes), 1)
    part, parity = lane // per, lane % rows
    seen = jnp.zeros((1, lanes), jnp.int32)
    at = 0
    for x in range(row_n):
        for c in range(core_n):
            for y in range(far_n):
                for z in range(kvh_n):
                    line = (mem ^ (y * core_n + c)) * kvh_n + (kvh ^ z)
                    for r in range(rows):
                        value = texts[x][line, r]
                        seen = jnp.where((part == at) & (parity == r), value, seen)
                    at += 1
    for b in range(out.shape[0]):
        if b < frames:
            block = mem * frames + b
            end, video = jnp.int32(0), jnp.int32(0)
            for v in range(blocks_ref.shape[0]):
                end = end + blocks_ref[v]
                video = video + (end <= block).astype(jnp.int32)
            out[b : b + 1, :] = jnp.where(video <= seen, 0.0, hidden).astype(f32)
        else:
            out[b : b + 1, :] = jnp.zeros((1, lanes), f32)


def gathered(refs, kvh_n, rows, head, which):
    per = GROUP * rows
    step = refs[0].shape[0] // kvh_n
    base = which * (step // 2) + head * per
    return jnp.concatenate(
        [ref[z * step + base : z * step + base + per, :] for ref in refs for z in range(kvh_n)],
        axis=0,
    )


def forward(count, own, kvh_n, rows, key_heads, frames, *refs):
    x_refs = refs[:count]
    k_ref, v_ref, vis, keep, send, stats, s_ref, p_ref = refs[count:]
    lanes = s_ref.shape[1]
    half = own // 2
    stat_rows = []
    for g in range(key_heads):
        query = gathered(x_refs, kvh_n, rows, g, 0)
        grad = gathered(x_refs, kvh_n, rows, g, 1)
        cols = slice(g * HEAD_WIDTH, (g + 1) * HEAD_WIDTH)
        top = jnp.full((1, lanes), masked_score, f32)
        for b in range(frames):
            at = slice(b * FRAME, (b + 1) * FRAME)
            scores = dot(k_ref[at, cols], query, NT)
            s_ref[at, :] = scores
            best = jnp.max(scores, axis=0, keepdims=True)
            top = jnp.maximum(top, jnp.where(vis[b : b + 1, :] == 0.0, best, masked_score))
        total = jnp.zeros((1, lanes), f32)
        dsum = jnp.zeros((1, lanes), f32)
        for b in range(frames):
            at = slice(b * FRAME, (b + 1) * FRAME)
            limit = jnp.where(vis[b : b + 1, :] == 0.0, top, hidden)
            weight = jnp.exp2((s_ref[at, :] - limit) * exp2_scale)
            prob_grad = dot(v_ref[at, cols], grad, NT)
            total = total + jnp.sum(weight, axis=0, keepdims=True)
            dsum = dsum + jnp.sum(weight * prob_grad, axis=0, keepdims=True)
            s_ref[at, :own] = weight[:, :own]
            p_ref[at, :] = prob_grad[:, :own]
        delta = jnp.where(total > 0.0, dsum / jnp.where(total > 0.0, total, 1.0), 0.0)
        stat_rows += [top, total, delta, jnp.zeros_like(top)]
        weight = s_ref[:, :own]
        change = (weight * (p_ref[...] - delta[:, :own])).astype(bf16)
        weight = weight.astype(bf16)
        num = dot(weight, v_ref[:, cols], TN)
        mean = dot(weight, k_ref[:, cols], TN)
        part = dot(change, k_ref[:, cols], TN)
        for n, value in enumerate((num, part, mean)):
            line = (n * key_heads + g) * half
            keep[line : line + half, :] = value[:half, :].astype(bf16)
            send[line : line + half, :] = value[half:, :].astype(bf16)
    stats[...] = jnp.concatenate(stat_rows, axis=0)


def merged(stats, other, g):
    top1, total1, delta1 = (stats[4 * g + i : 4 * g + i + 1, :] for i in range(3))
    top2, total2, delta2 = (other[4 * g + i : 4 * g + i + 1, :] for i in range(3))
    top = jnp.maximum(top1, top2)
    e1 = jnp.exp2((top1 - top) * exp2_scale)
    e2 = jnp.exp2((top2 - top) * exp2_scale)
    m1, m2 = e1 * total1, e2 * total2
    total = m1 + m2
    safe = jnp.where(total > 0.0, total, 1.0)
    delta = (m1 * delta1 + m2 * delta2) / safe
    return top, total, delta, e1, e2, e1 * (delta - delta1), e2 * (delta - delta2)


def merge(final, swap, used, kvh_n, key_heads, keep, got, stats, other, *outs):
    lanes = stats.shape[1]
    other = other[...]
    pieces = []
    for at in range(0, lanes, 2 * swap):
        pieces += [other[:, at + swap : at + 2 * swap], other[:, at : at + swap]]
    other = jnp.concatenate(pieces, axis=1)
    mine = stats[...]
    stat_rows = []
    for g in range(key_heads):
        top, total, delta, e1, e2, d1, d2 = merged(mine, other, g)
        if final:
            log2 = top + jnp.log2(total) * (1.0 / exp2_scale)
            stat_rows += [log2, delta, jnp.zeros_like(top), jnp.zeros_like(top)]
            scale = 1.0 / total
            e1, e2, d1, d2 = e1 * scale, e2 * scale, d1 * scale, d2 * scale
        else:
            stat_rows += [top, total, delta, jnp.zeros_like(top)]
        columns = jnp.concatenate([e1, e2, d1, d2, e1, e2, d1, d2], axis=0)[:, :HEAD_WIDTH].T
        e1, e2, d1, d2 = (columns[:used, i : i + 1] for i in range(4))

        def side(ref, n):
            line = (n * key_heads + g) * used
            return ref[line : line + used, :].astype(f32)

        mean1, mean2 = side(keep, 2), side(got, 2)
        num = e1 * side(keep, 0) + e2 * side(got, 0)
        part = e1 * side(keep, 1) - d1 * mean1 + (e2 * side(got, 1) - d2 * mean2)
        if final:
            per = used // kvh_n
            for z in range(kvh_n):
                for n, value in enumerate((num, part * inverse_root)):
                    line = (n * key_heads + g) * per
                    outs[z][line : line + per, :] = value[z * per : (z + 1) * per, :].astype(bf16)
        else:
            half = used // 2
            mean = e1 * mean1 + e2 * mean2
            for n, value in enumerate((num, part, mean)):
                line = (n * key_heads + g) * half
                outs[0][line : line + half, :] = value[:half, :].astype(bf16)
                outs[1][line : line + half, :] = value[half:, :].astype(bf16)
    outs[-1][...] = jnp.concatenate(stat_rows, axis=0)


def backward(count, kvh_n, rows, key_heads, frames, *refs):
    x_refs = refs[:count]
    k_ref, v_ref, vis, stats, dk_ref, dv_ref = refs[count:]
    for g in range(key_heads):
        query = gathered(x_refs, kvh_n, rows, g, 0)
        grad = gathered(x_refs, kvh_n, rows, g, 1)
        cols = slice(g * HEAD_WIDTH, (g + 1) * HEAD_WIDTH)
        log_mass = stats[4 * g : 4 * g + 1, :]
        delta = stats[4 * g + 1 : 4 * g + 2, :]
        for b in range(frames):
            at = slice(b * FRAME, (b + 1) * FRAME)
            limit = jnp.where(vis[b : b + 1, :] == 0.0, log_mass, hidden)
            scores = dot(k_ref[at, cols], query, NT)
            probability = jnp.exp2((scores - limit) * exp2_scale)
            prob_grad = dot(v_ref[at, cols], grad, NT)
            score_grad = (probability * (prob_grad - delta)).astype(bf16)
            dk_ref[at, cols] = (dot(score_grad, query, NN) * inverse_root).astype(bf16)
            dv_ref[at, cols] = dot(probability.astype(bf16), grad, NN).astype(bf16)


def exchange(x, axes, count, d):
    return lax.ppermute(x, axes, [(i, i ^ d) for i in range(count)])


def direct(sizes, queries, output_gradient, keys, values, text_video, video_blocks):
    mem_n, kvh_n, row_n = sizes
    core_n, far_n = 2, mem_n // 2
    rows = queries.shape[0]
    key_heads = keys.shape[1] // HEAD_WIDTH
    frames = keys.shape[0] // FRAME
    per = GROUP * rows
    block = 2 * key_heads * per
    own = mem_n * kvh_n * per
    lanes = row_n * own
    where = jnp.stack([lax.axis_index("kvh"), lax.axis_index("mem")]).astype(jnp.int32)

    def shape(n, m=HEAD_WIDTH, kind=bf16):
        return jax.ShapeDtypeStruct((n, m), kind)

    parts = call(
        functools.partial(split_columns, kvh_n, rows),
        [shape(block)] * kvh_n,
        [SM, VM, VM],
        [pltpu.VMEM((block, HEAD_WIDTH), f32)],
        moved=4 * queries.size,
    )(where, queries, output_gradient)
    parts = [parts[0]] + [exchange(parts[d], "kvh", kvh_n, d) for d in range(1, kvh_n)]
    column = jnp.concatenate(parts, axis=0)

    texts = [text_video] + [exchange(text_video, "row", row_n, x) for x in range(1, row_n)]
    vis = call(
        functools.partial(visibility, (row_n, core_n, far_n, kvh_n, rows, frames)),
        shape(-(-frames // 8) * 8, lanes, f32),
        [SM, SM] + [SM] * row_n,
        moved=4 * lanes * 8,
    )(where, video_blocks, *texts)

    near = {}
    for x in range(row_n):
        for y in range(far_n):
            d = y * core_n * row_n + x
            near[x, y] = exchange(column, ("mem", "row"), mem_n * row_n, d) if d else column
    x_all = []
    for x in range(row_n):
        for c in range(core_n):
            for y in range(far_n):
                x_all.append(exchange(near[x, y], "mem", mem_n, 1) if c else near[x, y])

    count = len(x_all)
    half = own // 2
    tokens = keys.shape[0]
    work = 2 * tokens * HEAD_WIDTH * key_heads
    keep, send, stats = call(
        functools.partial(forward, count, own, kvh_n, rows, key_heads, frames),
        [shape(3 * key_heads * half), shape(3 * key_heads * half), shape(4 * key_heads, lanes, f32)],
        [VM] * (count + 3),
        [pltpu.VMEM((tokens, lanes), f32), pltpu.VMEM((tokens, own), f32)],
        flops=work * (2 * lanes + 3 * own),
        exps=tokens * lanes * key_heads,
        moved=4 * keys.size,
    )(*x_all, keys, values, vis)

    got, other = exchange(send, "mem", mem_n, 1), exchange(stats, "mem", mem_n, 1)
    half = half // 2
    keep, send, stats = call(
        functools.partial(merge, False, own // 2, own // 2, kvh_n, key_heads),
        [shape(3 * key_heads * half), shape(3 * key_heads * half), shape(4 * key_heads, lanes, f32)],
        [VM] * 4,
        moved=4 * keep.size,
    )(keep, got, stats, other)

    got, other = exchange(send, "mem", mem_n, 2), exchange(stats, "mem", mem_n, 2)
    *parts, stats = call(
        functools.partial(merge, True, half, half, kvh_n, key_heads),
        [shape(block)] * kvh_n + [shape(4 * key_heads, lanes, f32)],
        [VM] * 4,
        moved=4 * keep.size,
    )(keep, got, stats, other)

    parts = [parts[0]] + [exchange(parts[d], "kvh", kvh_n, d) for d in range(1, kvh_n)]
    keys_gradient, values_gradient = call(
        functools.partial(backward, count, kvh_n, rows, key_heads, frames),
        [jax.ShapeDtypeStruct(keys.shape, bf16)] * 2,
        [VM] * (count + 4),
        flops=work * 4 * lanes,
        exps=tokens * lanes * key_heads,
        moved=8 * keys.size,
    )(*x_all, keys, values, vis, stats)
    attention_out, query_grad = call(
        functools.partial(join_columns, kvh_n, rows),
        [jax.ShapeDtypeStruct(queries.shape, bf16)] * 2,
        [SM] + [VM] * kvh_n,
        [pltpu.VMEM((block, HEAD_WIDTH), f32)],
        moved=4 * queries.size,
    )(where, *parts)
    return attention_out, query_grad, keys_gradient, values_gradient


def video_of_block(video_blocks, first_block, block_count):
    block_ends = jnp.cumsum(video_blocks)
    blocks = first_block + jnp.arange(block_count, dtype=jnp.int32)
    return jnp.sum((block_ends[None, :] <= blocks[:, None]).astype(jnp.int32), axis=1)


def general(queries, output_gradient, keys, values, text_video, video_blocks):
    inverse_root = HEAD_WIDTH ** (-0.5)
    heads_per_group = QUERY_HEADS // KEY_VALUE_HEADS
    mem_count = lax.axis_size("mem")
    local_query, local_grad = (
        lax.all_to_all(queries, "kvh", split_axis=1, concat_axis=0, tiled=True),
        lax.all_to_all(output_gradient, "kvh", split_axis=1, concat_axis=0, tiled=True),
    )
    query_rows, grad_rows = (
        lax.all_gather(local_query, "mem", axis=0, tiled=True),
        lax.all_gather(local_grad, "mem", axis=0, tiled=True),
    )
    group_size = query_rows.shape[0]
    own_count = local_query.shape[0]
    key_local = keys.shape[1] // HEAD_WIDTH
    frames = keys.shape[0] // FRAME
    query_four = query_rows.reshape(group_size, key_local, heads_per_group, HEAD_WIDTH)
    grad_four = grad_rows.reshape(group_size, key_local, heads_per_group, HEAD_WIDTH)
    key_frames = keys.reshape(frames, FRAME, key_local, HEAD_WIDTH)
    value_frames = values.reshape(frames, FRAME, key_local, HEAD_WIDTH)
    key_video = video_of_block(video_blocks, lax.axis_index("mem") * frames, frames)
    visible = key_video[None, :] <= text_video.reshape(group_size)[:, None]
    frame_ids = jnp.arange(frames, dtype=jnp.int32)

    def frame_scores(frame_index):
        key_block = lax.dynamic_index_in_dim(key_frames, frame_index, 0, keepdims=False)
        scores = (
            jnp.einsum("rghd,jgd->rghj", query_four, key_block, preferred_element_type=jnp.float32)
            * inverse_root
        )
        seen_rows = lax.dynamic_index_in_dim(visible, frame_index, 1, keepdims=False)[
            :, None, None, None
        ]
        return (jnp.where(seen_rows, scores, masked_score), seen_rows, key_block)

    def forward_step(running, frame_index):
        running_top, totals, numerator = running
        scores, seen_rows, key_block = frame_scores(frame_index)
        new_top = jnp.maximum(running_top, jnp.max(scores, axis=3))
        weight = jnp.where(seen_rows, jnp.exp(scores - new_top[..., None]), 0.0)
        shrink_factor = jnp.exp(running_top - new_top)
        totals = totals * shrink_factor + jnp.sum(weight, axis=3)
        value_block = lax.dynamic_index_in_dim(value_frames, frame_index, 0, keepdims=False)
        numerator = numerator * shrink_factor[..., None] + jnp.einsum(
            "rghj,jgd->rghd",
            weight.astype(jnp.bfloat16),
            value_block,
            preferred_element_type=jnp.float32,
        )
        return ((new_top, totals, numerator), None)

    stat_shape = (group_size, key_local, heads_per_group)
    start_state = (
        jnp.full(stat_shape, masked_score, jnp.float32),
        jnp.zeros(stat_shape, jnp.float32),
        jnp.zeros(stat_shape + (HEAD_WIDTH,), jnp.float32),
    )
    (local_top, local_totals, numerator), unused = lax.scan(forward_step, start_state, frame_ids)
    own_grad = local_grad.reshape(own_count, key_local, heads_per_group, HEAD_WIDTH).astype(
        jnp.float32
    )
    sent = (
        numerator.reshape((mem_count, own_count) + numerator.shape[1:]),
        local_top.reshape((mem_count, own_count) + stat_shape[1:]),
        local_totals.reshape((mem_count, own_count) + stat_shape[1:]),
    )
    numerator_src, top_src, totals_src = (
        lax.all_to_all(sent[0], "mem", split_axis=0, concat_axis=0, tiled=True),
        lax.all_to_all(sent[1], "mem", split_axis=0, concat_axis=0, tiled=True),
        lax.all_to_all(sent[2], "mem", split_axis=0, concat_axis=0, tiled=True),
    )
    own_top = jnp.max(top_src, axis=0)
    factor = jnp.exp(top_src - own_top)
    own_totals = jnp.sum(totals_src * factor, axis=0)
    attention = jnp.sum(numerator_src * factor[..., None], axis=0) / own_totals[..., None]
    delta_own = jnp.sum(own_grad * attention, axis=3)
    own_log = own_top + jnp.log(own_totals)
    log_mass, delta_rows = (
        lax.all_gather(own_log, "mem", axis=0, tiled=True),
        lax.all_gather(delta_own, "mem", axis=0, tiled=True),
    )
    attention_low = attention.reshape(own_count, key_local * heads_per_group * HEAD_WIDTH).astype(
        jnp.bfloat16
    )

    def backward_step(query_grad, frame_index):
        scores, seen_rows, key_block = frame_scores(frame_index)
        value_block = lax.dynamic_index_in_dim(value_frames, frame_index, 0, keepdims=False)
        probability = jnp.where(seen_rows, jnp.exp(scores - log_mass[..., None]), 0.0)
        prob_grad = jnp.einsum(
            "rghd,jgd->rghj", grad_four, value_block, preferred_element_type=jnp.float32
        )
        score_grad = (probability * (prob_grad - delta_rows[..., None])).astype(jnp.bfloat16)
        query_grad = (
            query_grad
            + jnp.einsum(
                "rghj,jgd->rghd", score_grad, key_block, preferred_element_type=jnp.float32
            )
            * inverse_root
        )
        key_part = (
            jnp.einsum("rghj,rghd->jgd", score_grad, query_four, preferred_element_type=jnp.float32)
            * inverse_root
        )
        value_part = jnp.einsum(
            "rghj,rghd->jgd",
            probability.astype(jnp.bfloat16),
            grad_four,
            preferred_element_type=jnp.float32,
        )
        return (query_grad, (key_part, value_part))

    query_grad, (key_parts, value_parts) = lax.scan(
        backward_step, jnp.zeros(stat_shape + (HEAD_WIDTH,), jnp.float32), frame_ids
    )
    key_sum = key_parts.reshape(keys.shape)
    value_sum = value_parts.reshape(values.shape)
    key_sum, value_sum = (
        lax.psum(key_sum.astype(jnp.bfloat16), "row").astype(jnp.float32),
        lax.psum(value_sum.astype(jnp.bfloat16), "row").astype(jnp.float32),
    )
    own_query_grad = lax.psum_scatter(
        query_grad.astype(jnp.bfloat16), "mem", scatter_dimension=0, tiled=True
    ).astype(jnp.float32)
    query_low = own_query_grad.reshape(own_count, key_local * heads_per_group * HEAD_WIDTH).astype(
        jnp.bfloat16
    )
    attention_text, query_text = (
        lax.all_to_all(attention_low, "kvh", split_axis=0, concat_axis=1, tiled=True),
        lax.all_to_all(query_low, "kvh", split_axis=0, concat_axis=1, tiled=True),
    )
    return (
        attention_text,
        query_text,
        key_sum.astype(jnp.bfloat16),
        value_sum.astype(jnp.bfloat16),
    )


def solution(mesh):
    in_specs = (
        P(("mem", "kvh", "row"), None),
        P(("mem", "kvh", "row"), None),
        P("mem", "kvh"),
        P("mem", "kvh"),
        P(None, "row"),
        P(),
    )
    out_specs = (
        P(("mem", "kvh", "row"), None),
        P(("mem", "kvh", "row"), None),
        P("mem", "kvh"),
        P("mem", "kvh"),
    )
    sizes = tuple(mesh.shape[axis] for axis in ("mem", "kvh", "row"))
    body = functools.partial(direct, sizes) if sizes[0] == 4 else general
    return jax.shard_map(
        body, mesh=mesh, in_specs=in_specs, out_specs=out_specs, check_vma=False
    )
```

```python
import functools
import math

import jax
import jax.numpy as jnp
from jax import lax
from jax.experimental import pallas as pl
from jax.experimental.pallas import tpu as pltpu
from jax.sharding import PartitionSpec as P

QUERY_HEADS = 64
KEY_VALUE_HEADS = 8
HEAD_WIDTH = 128
FRAME = 128
GROUP = QUERY_HEADS // KEY_VALUE_HEADS


masked_score = -1e30
hidden = 1e30
inverse_root = HEAD_WIDTH ** (-0.5)
exp2_scale = inverse_root * math.log2(math.e)

NT = (((1,), (1,)), ((), ()))
NN = (((1,), (0,)), ((), ()))
TN = (((0,), (0,)), ((), ()))
VM = pl.BlockSpec(memory_space=pltpu.VMEM)
SM = pl.BlockSpec(memory_space=pltpu.SMEM)
HB = pl.BlockSpec(memory_space=pl.ANY)
f32 = jnp.float32
bf16 = jnp.bfloat16


def dot(a, b, dims):
    return lax.dot_general(a, b, dims, preferred_element_type=f32)


def call(body, outs, specs, scratch=(), flops=0, exps=0, moved=0, outside=False):
    return pl.pallas_call(
        body,
        out_shape=outs,
        in_specs=specs,
        out_specs=jax.tree.map(lambda _: HB if outside else VM, outs),
        scratch_shapes=list(scratch),
        cost_estimate=pl.CostEstimate(
            flops=flops, transcendentals=exps, bytes_accessed=moved
        ),
        compiler_params=pltpu.CompilerParams(vmem_limit_bytes=40 << 20),
    )


def split_columns(parts, rows, q_any, g_any, *rest):
    outs = rest[:parts]
    q_ref, g_ref, tmp, sems = rest[parts:]
    copies = [
        pltpu.make_async_copy(source, ref, sems.at[n])
        for n, (source, ref) in enumerate(((q_any, q_ref), (g_any, g_ref)))
    ]
    for copy in copies:
        copy.start()
    heads = q_ref.shape[1] // HEAD_WIDTH // parts
    own = lax.axis_index("kvh")
    for n, ref in enumerate((q_ref, g_ref)):
        copies[n].wait()
        for d in range(parts):
            base = (own ^ d) * (heads * HEAD_WIDTH)
            for h in range(heads):
                at = pl.multiple_of(base + h * HEAD_WIDTH, HEAD_WIDTH)
                line = ((d * 2 + n) * heads + h) * rows
                tmp[line : line + rows, :] = ref[:, pl.ds(at, HEAD_WIDTH)].astype(f32)
    size = 2 * heads * rows
    for d in range(parts):
        outs[d][...] = tmp[d * size : (d + 1) * size, :].astype(bf16)


def join_columns(parts, rows, *rest):
    blocks, outs = rest[:parts], rest[parts : parts + 2]
    a_ref, q_ref, tmp, sems = rest[parts + 2 :]
    heads = q_ref.shape[1] // HEAD_WIDTH // parts
    own = lax.axis_index("kvh")
    size = 2 * heads * rows
    for d in range(parts):
        tmp[d * size : (d + 1) * size, :] = blocks[d][...].astype(f32)
    copies = []
    for n, ref in enumerate((a_ref, q_ref)):
        for d in range(parts):
            base = (own ^ d) * (heads * HEAD_WIDTH)
            for h in range(heads):
                at = pl.multiple_of(base + h * HEAD_WIDTH, HEAD_WIDTH)
                line = ((d * 2 + n) * heads + h) * rows
                ref[:, pl.ds(at, HEAD_WIDTH)] = tmp[line : line + rows, :].astype(bf16)
        copy = pltpu.make_async_copy(ref, outs[n], sems.at[n])
        copy.start()
        copies.append(copy)
    for copy in copies:
        copy.wait()


def stack(count, *refs):
    out = refs[count + 1]
    size = refs[0].shape[0]
    for d in range(count):
        out[d * size : (d + 1) * size, :] = refs[d][...]


def prepare(sizes, blocks_ref, k_any, v_any, *rest):
    row_n, core_n, far_n, kvh_n, rows, frames = sizes
    texts = rest[:row_n]
    out, k_ref, v_ref, sems = rest[row_n:]
    copies = [
        pltpu.make_async_copy(source, ref, sems.at[n])
        for n, (source, ref) in enumerate(((k_any, k_ref), (v_any, v_ref)))
    ]
    for copy in copies:
        copy.start()
    kvh, mem = lax.axis_index("kvh"), lax.axis_index("mem")
    lanes = out.shape[1]
    per = GROUP * rows
    lane = lax.broadcasted_iota(jnp.int32, (1, lanes), 1)
    part, parity = lane // per, lane % rows
    seen = jnp.zeros((1, lanes), jnp.int32)
    at = 0
    for x in range(row_n):
        for c in range(core_n):
            for y in range(far_n):
                for z in range(kvh_n):
                    line = (mem ^ (y * core_n + c)) * kvh_n + (kvh ^ z)
                    for r in range(rows):
                        value = texts[x][line, r]
                        seen = jnp.where((part == at) & (parity == r), value, seen)
                    at += 1
    for b in range(out.shape[0]):
        if b < frames:
            block = mem * frames + b
            end, video = jnp.int32(0), jnp.int32(0)
            for v in range(blocks_ref.shape[0]):
                end = end + blocks_ref[v]
                video = video + (end <= block).astype(jnp.int32)
            out[b : b + 1, :] = jnp.where(video <= seen, 0.0, hidden).astype(f32)
        else:
            out[b : b + 1, :] = jnp.zeros((1, lanes), f32)
    for copy in copies:
        copy.wait()


def gathered(refs, kvh_n, rows, head, which):
    per = GROUP * rows
    step = refs[0].shape[0] // kvh_n
    base = which * (step // 2) + head * per
    return jnp.concatenate(
        [ref[z * step + base : z * step + base + per, :] for ref in refs for z in range(kvh_n)],
        axis=0,
    )


def forward(count, own, kvh_n, rows, key_heads, frames, *refs):
    x_refs = refs[:count]
    k_ref, v_ref, vis, keep, send, stats, s_ref, p_ref = refs[count:]
    tokens = k_ref.shape[0]
    lanes = s_ref.shape[1]
    half = own // 2
    stat_rows = []
    for g in range(key_heads):
        query = gathered(x_refs, kvh_n, rows, g, 0)
        grad = gathered(x_refs, kvh_n, rows, g, 1)
        cols = slice(g * HEAD_WIDTH, (g + 1) * HEAD_WIDTH)
        base = g * tokens
        top = jnp.full((1, lanes), masked_score, f32)
        for b in range(frames):
            at = slice(b * FRAME, (b + 1) * FRAME)
            scores = dot(k_ref[at, cols], query, NT)
            s_ref[base + b * FRAME : base + (b + 1) * FRAME, :] = scores
            best = jnp.max(scores, axis=0, keepdims=True)
            top = jnp.maximum(top, jnp.where(vis[b : b + 1, :] == 0.0, best, masked_score))
        total = jnp.zeros((1, lanes), f32)
        dsum = jnp.zeros((1, lanes), f32)
        for b in range(frames):
            at = slice(b * FRAME, (b + 1) * FRAME)
            to = slice(base + b * FRAME, base + (b + 1) * FRAME)
            limit = jnp.where(vis[b : b + 1, :] == 0.0, top, hidden)
            weight = jnp.exp2((s_ref[to, :] - limit) * exp2_scale)
            prob_grad = dot(v_ref[at, cols], grad, NT)
            total = total + jnp.sum(weight, axis=0, keepdims=True)
            dsum = dsum + jnp.sum(weight * prob_grad, axis=0, keepdims=True)
            s_ref[to, :] = weight
            p_ref[to, :] = prob_grad
        delta = jnp.where(total > 0.0, dsum / jnp.where(total > 0.0, total, 1.0), 0.0)
        stat_rows += [top, total, delta, jnp.zeros_like(top)]
        weight = s_ref[base : base + tokens, :own]
        change = (weight * (p_ref[base : base + tokens, :own] - delta[:, :own])).astype(bf16)
        weight = weight.astype(bf16)
        num = dot(weight, v_ref[:, cols], TN)
        mean = dot(weight, k_ref[:, cols], TN)
        part = dot(change, k_ref[:, cols], TN)
        for n, value in enumerate((num, part, mean)):
            line = (n * key_heads + g) * half
            keep[line : line + half, :] = value[:half, :].astype(bf16)
            send[line : line + half, :] = value[half:, :].astype(bf16)
    stats[...] = jnp.concatenate(stat_rows, axis=0)


def merged(stats, other, g):
    top1, total1, delta1 = (stats[4 * g + i : 4 * g + i + 1, :] for i in range(3))
    top2, total2, delta2 = (other[4 * g + i : 4 * g + i + 1, :] for i in range(3))
    top = jnp.maximum(top1, top2)
    e1 = jnp.exp2((top1 - top) * exp2_scale)
    e2 = jnp.exp2((top2 - top) * exp2_scale)
    m1, m2 = e1 * total1, e2 * total2
    total = m1 + m2
    safe = jnp.where(total > 0.0, total, 1.0)
    delta = (m1 * delta1 + m2 * delta2) / safe
    return top, total, delta, e1, e2, e1 * (delta - delta1), e2 * (delta - delta2)


def merge(final, swap, used, kvh_n, key_heads, keep, got, stats, other, *outs):
    lanes = stats.shape[1]
    other = other[...]
    pieces = []
    for at in range(0, lanes, 2 * swap):
        pieces += [other[:, at + swap : at + 2 * swap], other[:, at : at + swap]]
    other = jnp.concatenate(pieces, axis=1)
    mine = stats[...]
    stat_rows = []
    for g in range(key_heads):
        top, total, delta, e1, e2, d1, d2 = merged(mine, other, g)
        if final:
            log2 = top + jnp.log2(total) * (1.0 / exp2_scale)
            stat_rows += [log2, delta, jnp.zeros_like(top), jnp.zeros_like(top)]
            scale = 1.0 / total
            e1, e2, d1, d2 = e1 * scale, e2 * scale, d1 * scale, d2 * scale
        else:
            stat_rows += [top, total, delta, jnp.zeros_like(top)]
        columns = jnp.concatenate([e1, e2, d1, d2, e1, e2, d1, d2], axis=0)[:, :HEAD_WIDTH].T
        e1, e2, d1, d2 = (columns[:used, i : i + 1] for i in range(4))

        def side(ref, n):
            line = (n * key_heads + g) * used
            return ref[line : line + used, :].astype(f32)

        mean1, mean2 = side(keep, 2), side(got, 2)
        num = e1 * side(keep, 0) + e2 * side(got, 0)
        part = e1 * side(keep, 1) - d1 * mean1 + (e2 * side(got, 1) - d2 * mean2)
        if final:
            per = used // kvh_n
            for z in range(kvh_n):
                for n, value in enumerate((num, part * inverse_root)):
                    line = (n * key_heads + g) * per
                    outs[z][line : line + per, :] = value[z * per : (z + 1) * per, :].astype(bf16)
        else:
            half = used // 2
            mean = e1 * mean1 + e2 * mean2
            for n, value in enumerate((num, part, mean)):
                line = (n * key_heads + g) * half
                outs[0][line : line + half, :] = value[:half, :].astype(bf16)
                outs[1][line : line + half, :] = value[half:, :].astype(bf16)
    outs[-1][...] = jnp.concatenate(stat_rows, axis=0)


def backward(count, kvh_n, rows, key_heads, frames, *refs):
    x_refs = refs[:count]
    w_ref, p_ref, local, stats, dk_any, dv_any, dk_ref, dv_ref, sems = refs[count:]
    tokens = dk_ref.shape[0]
    query = [gathered(x_refs, kvh_n, rows, g, 0) for g in range(key_heads)]
    grad = [gathered(x_refs, kvh_n, rows, g, 1) for g in range(key_heads)]
    factor, delta = [], []
    for g in range(key_heads):
        top = local[4 * g : 4 * g + 1, :]
        factor.append(jnp.exp2((top - stats[4 * g : 4 * g + 1, :]) * exp2_scale))
        delta.append(stats[4 * g + 1 : 4 * g + 2, :])
    copies = []
    for b in range(frames):
        at = slice(b * FRAME, (b + 1) * FRAME)
        for g in range(key_heads):
            cols = slice(g * HEAD_WIDTH, (g + 1) * HEAD_WIDTH)
            of = slice(g * tokens + b * FRAME, g * tokens + (b + 1) * FRAME)
            probability = w_ref[of, :] * factor[g]
            score_grad = (probability * (p_ref[of, :] - delta[g])).astype(bf16)
            dk_ref[at, cols] = (dot(score_grad, query[g], NN) * inverse_root).astype(bf16)
            dv_ref[at, cols] = dot(probability.astype(bf16), grad[g], NN).astype(bf16)
        for n, (ref, out) in enumerate(((dk_ref, dk_any), (dv_ref, dv_any))):
            copy = pltpu.make_async_copy(ref.at[at], out.at[at], sems.at[n, b])
            copy.start()
            copies.append(copy)
    for copy in copies:
        copy.wait()


def exchange(x, axes, count, d):
    return lax.ppermute(x, axes, [(i, i ^ d) for i in range(count)])


def direct(sizes, queries, output_gradient, keys, values, text_video, video_blocks):
    mem_n, kvh_n, row_n = sizes
    core_n, far_n = 2, mem_n // 2
    rows = queries.shape[0]
    key_heads = keys.shape[1] // HEAD_WIDTH
    frames = keys.shape[0] // FRAME
    per = GROUP * rows
    block = 2 * key_heads * per
    own = mem_n * kvh_n * per
    lanes = row_n * own
    tokens = keys.shape[0]
    dma = pltpu.SemaphoreType.DMA

    def shape(n, m=HEAD_WIDTH, kind=bf16):
        return jax.ShapeDtypeStruct((n, m), kind)

    parts = call(
        functools.partial(split_columns, kvh_n, rows),
        [shape(block)] * kvh_n,
        [HB, HB],
        [pltpu.VMEM(queries.shape, bf16)] * 2
        + [pltpu.VMEM((kvh_n * block, HEAD_WIDTH), f32), dma((2,))],
        moved=4 * queries.size,
    )(queries, output_gradient)
    parts = [parts[0]] + [exchange(parts[d], "kvh", kvh_n, d) for d in range(1, kvh_n)]

    texts = [text_video] + [exchange(text_video, "row", row_n, x) for x in range(1, row_n)]
    vis, keys, values = call(
        functools.partial(prepare, (row_n, core_n, far_n, kvh_n, rows, frames)),
        [shape(-(-frames // 8) * 8, lanes, f32)] + [shape(*keys.shape)] * 2,
        [SM, HB, HB] + [SM] * row_n,
        [dma((2,))],
        moved=4 * keys.size,
    )(video_blocks, keys, values, *texts)
    column = call(
        functools.partial(stack, kvh_n), shape(kvh_n * block), [VM] * kvh_n + [HB]
    )(*parts, vis)

    near = {}
    for x in range(row_n):
        for y in range(far_n):
            d = y * core_n * row_n + x
            near[x, y] = exchange(column, ("mem", "row"), mem_n * row_n, d) if d else column
    x_all = []
    for x in range(row_n):
        for c in range(core_n):
            for y in range(far_n):
                x_all.append(exchange(near[x, y], "mem", mem_n, 1) if c else near[x, y])

    count = len(x_all)
    half = own // 2
    work = 2 * tokens * HEAD_WIDTH * key_heads
    keep, send, local, weight, prob_grad = call(
        functools.partial(forward, count, own, kvh_n, rows, key_heads, frames),
        [shape(3 * key_heads * half)] * 2
        + [shape(4 * key_heads, lanes, f32)]
        + [shape(key_heads * tokens, lanes, f32)] * 2,
        [VM] * (count + 3),
        flops=work * (2 * lanes + 3 * own),
        exps=tokens * lanes * key_heads,
        moved=4 * keys.size,
    )(*x_all, keys, values, vis)

    got, other = exchange(send, "mem", mem_n, 1), exchange(local, "mem", mem_n, 1)
    half = half // 2
    keep, send, stats = call(
        functools.partial(merge, False, own // 2, own // 2, kvh_n, key_heads),
        [shape(3 * key_heads * half), shape(3 * key_heads * half), shape(4 * key_heads, lanes, f32)],
        [VM] * 4,
        moved=4 * keep.size,
    )(keep, got, local, other)

    got, other = exchange(send, "mem", mem_n, 2), exchange(stats, "mem", mem_n, 2)
    *parts, stats = call(
        functools.partial(merge, True, half, half, kvh_n, key_heads),
        [shape(block)] * kvh_n + [shape(4 * key_heads, lanes, f32)],
        [VM] * 4,
        moved=4 * keep.size,
    )(keep, got, stats, other)

    parts = [parts[0]] + [exchange(parts[d], "kvh", kvh_n, d) for d in range(1, kvh_n)]
    keys_gradient, values_gradient = call(
        functools.partial(backward, count, kvh_n, rows, key_heads, frames),
        [shape(*keys.shape)] * 2,
        [VM] * (count + 4),
        [pltpu.VMEM(keys.shape, bf16)] * 2 + [dma((2, frames))],
        flops=work * 2 * lanes,
        moved=4 * keys.size,
        outside=True,
    )(*x_all, weight, prob_grad, local, stats)
    attention_out, query_grad = call(
        functools.partial(join_columns, kvh_n, rows),
        [shape(*queries.shape)] * 2,
        [VM] * kvh_n,
        [pltpu.VMEM(queries.shape, bf16)] * 2
        + [pltpu.VMEM((kvh_n * block, HEAD_WIDTH), f32), dma((2,))],
        moved=4 * queries.size,
        outside=True,
    )(*parts)
    return attention_out, query_grad, keys_gradient, values_gradient


def video_of_block(video_blocks, first_block, block_count):
    block_ends = jnp.cumsum(video_blocks)
    blocks = first_block + jnp.arange(block_count, dtype=jnp.int32)
    return jnp.sum((block_ends[None, :] <= blocks[:, None]).astype(jnp.int32), axis=1)


def general(queries, output_gradient, keys, values, text_video, video_blocks):
    inverse_root = HEAD_WIDTH ** (-0.5)
    heads_per_group = QUERY_HEADS // KEY_VALUE_HEADS
    mem_count = lax.axis_size("mem")
    local_query, local_grad = (
        lax.all_to_all(queries, "kvh", split_axis=1, concat_axis=0, tiled=True),
        lax.all_to_all(output_gradient, "kvh", split_axis=1, concat_axis=0, tiled=True),
    )
    query_rows, grad_rows = (
        lax.all_gather(local_query, "mem", axis=0, tiled=True),
        lax.all_gather(local_grad, "mem", axis=0, tiled=True),
    )
    group_size = query_rows.shape[0]
    own_count = local_query.shape[0]
    key_local = keys.shape[1] // HEAD_WIDTH
    frames = keys.shape[0] // FRAME
    query_four = query_rows.reshape(group_size, key_local, heads_per_group, HEAD_WIDTH)
    grad_four = grad_rows.reshape(group_size, key_local, heads_per_group, HEAD_WIDTH)
    key_frames = keys.reshape(frames, FRAME, key_local, HEAD_WIDTH)
    value_frames = values.reshape(frames, FRAME, key_local, HEAD_WIDTH)
    key_video = video_of_block(video_blocks, lax.axis_index("mem") * frames, frames)
    visible = key_video[None, :] <= text_video.reshape(group_size)[:, None]
    frame_ids = jnp.arange(frames, dtype=jnp.int32)

    def frame_scores(frame_index):
        key_block = lax.dynamic_index_in_dim(key_frames, frame_index, 0, keepdims=False)
        scores = (
            jnp.einsum("rghd,jgd->rghj", query_four, key_block, preferred_element_type=jnp.float32)
            * inverse_root
        )
        seen_rows = lax.dynamic_index_in_dim(visible, frame_index, 1, keepdims=False)[
            :, None, None, None
        ]
        return (jnp.where(seen_rows, scores, masked_score), seen_rows, key_block)

    def forward_step(running, frame_index):
        running_top, totals, numerator = running
        scores, seen_rows, key_block = frame_scores(frame_index)
        new_top = jnp.maximum(running_top, jnp.max(scores, axis=3))
        weight = jnp.where(seen_rows, jnp.exp(scores - new_top[..., None]), 0.0)
        shrink_factor = jnp.exp(running_top - new_top)
        totals = totals * shrink_factor + jnp.sum(weight, axis=3)
        value_block = lax.dynamic_index_in_dim(value_frames, frame_index, 0, keepdims=False)
        numerator = numerator * shrink_factor[..., None] + jnp.einsum(
            "rghj,jgd->rghd",
            weight.astype(jnp.bfloat16),
            value_block,
            preferred_element_type=jnp.float32,
        )
        return ((new_top, totals, numerator), None)

    stat_shape = (group_size, key_local, heads_per_group)
    start_state = (
        jnp.full(stat_shape, masked_score, jnp.float32),
        jnp.zeros(stat_shape, jnp.float32),
        jnp.zeros(stat_shape + (HEAD_WIDTH,), jnp.float32),
    )
    (local_top, local_totals, numerator), unused = lax.scan(forward_step, start_state, frame_ids)
    own_grad = local_grad.reshape(own_count, key_local, heads_per_group, HEAD_WIDTH).astype(
        jnp.float32
    )
    sent = (
        numerator.reshape((mem_count, own_count) + numerator.shape[1:]),
        local_top.reshape((mem_count, own_count) + stat_shape[1:]),
        local_totals.reshape((mem_count, own_count) + stat_shape[1:]),
    )
    numerator_src, top_src, totals_src = (
        lax.all_to_all(sent[0], "mem", split_axis=0, concat_axis=0, tiled=True),
        lax.all_to_all(sent[1], "mem", split_axis=0, concat_axis=0, tiled=True),
        lax.all_to_all(sent[2], "mem", split_axis=0, concat_axis=0, tiled=True),
    )
    own_top = jnp.max(top_src, axis=0)
    factor = jnp.exp(top_src - own_top)
    own_totals = jnp.sum(totals_src * factor, axis=0)
    attention = jnp.sum(numerator_src * factor[..., None], axis=0) / own_totals[..., None]
    delta_own = jnp.sum(own_grad * attention, axis=3)
    own_log = own_top + jnp.log(own_totals)
    log_mass, delta_rows = (
        lax.all_gather(own_log, "mem", axis=0, tiled=True),
        lax.all_gather(delta_own, "mem", axis=0, tiled=True),
    )
    attention_low = attention.reshape(own_count, key_local * heads_per_group * HEAD_WIDTH).astype(
        jnp.bfloat16
    )

    def backward_step(query_grad, frame_index):
        scores, seen_rows, key_block = frame_scores(frame_index)
        value_block = lax.dynamic_index_in_dim(value_frames, frame_index, 0, keepdims=False)
        probability = jnp.where(seen_rows, jnp.exp(scores - log_mass[..., None]), 0.0)
        prob_grad = jnp.einsum(
            "rghd,jgd->rghj", grad_four, value_block, preferred_element_type=jnp.float32
        )
        score_grad = (probability * (prob_grad - delta_rows[..., None])).astype(jnp.bfloat16)
        query_grad = (
            query_grad
            + jnp.einsum(
                "rghj,jgd->rghd", score_grad, key_block, preferred_element_type=jnp.float32
            )
            * inverse_root
        )
        key_part = (
            jnp.einsum("rghj,rghd->jgd", score_grad, query_four, preferred_element_type=jnp.float32)
            * inverse_root
        )
        value_part = jnp.einsum(
            "rghj,rghd->jgd",
            probability.astype(jnp.bfloat16),
            grad_four,
            preferred_element_type=jnp.float32,
        )
        return (query_grad, (key_part, value_part))

    query_grad, (key_parts, value_parts) = lax.scan(
        backward_step, jnp.zeros(stat_shape + (HEAD_WIDTH,), jnp.float32), frame_ids
    )
    key_sum = key_parts.reshape(keys.shape)
    value_sum = value_parts.reshape(values.shape)
    key_sum, value_sum = (
        lax.psum(key_sum.astype(jnp.bfloat16), "row").astype(jnp.float32),
        lax.psum(value_sum.astype(jnp.bfloat16), "row").astype(jnp.float32),
    )
    own_query_grad = lax.psum_scatter(
        query_grad.astype(jnp.bfloat16), "mem", scatter_dimension=0, tiled=True
    ).astype(jnp.float32)
    query_low = own_query_grad.reshape(own_count, key_local * heads_per_group * HEAD_WIDTH).astype(
        jnp.bfloat16
    )
    attention_text, query_text = (
        lax.all_to_all(attention_low, "kvh", split_axis=0, concat_axis=1, tiled=True),
        lax.all_to_all(query_low, "kvh", split_axis=0, concat_axis=1, tiled=True),
    )
    return (
        attention_text,
        query_text,
        key_sum.astype(jnp.bfloat16),
        value_sum.astype(jnp.bfloat16),
    )


def solution(mesh):
    in_specs = (
        P(("mem", "kvh", "row"), None),
        P(("mem", "kvh", "row"), None),
        P("mem", "kvh"),
        P("mem", "kvh"),
        P(None, "row"),
        P(),
    )
    out_specs = (
        P(("mem", "kvh", "row"), None),
        P(("mem", "kvh", "row"), None),
        P("mem", "kvh"),
        P("mem", "kvh"),
    )
    sizes = tuple(mesh.shape[axis] for axis in ("mem", "kvh", "row"))
    body = functools.partial(direct, sizes) if sizes[0] == 4 else general
    return jax.shard_map(
        body, mesh=mesh, in_specs=in_specs, out_specs=out_specs, check_vma=False
    )
```
